32 devices in a mesh: grp: 1, blk: 32 (over z, y, x, core).
Axes of the slice: x: 2, y: 2, z: 4, core: 2. Of those that a mesh axis runs over, the one named last changes fastest.
Arguments:
- activations: bfloat16 [4096, 8192], P(('grp', 'blk')), may hold values from -6 to 6
- out_grads: bfloat16 [4096, 28672], P(('grp', 'blk')), may hold values from -6 to 6
- query_factors: bfloat16 [384, 36864], P('blk'), may hold values from -0.046875 to 0.046875
- pair_query: int32 [384], replicated, may hold values from 0 to 11, as said below
- segment_ids: int32 [4096], P(('grp', 'blk')), may hold values from 0 to 3, never falling along the last dimension, each value on 1 to 2048 neighbouring positions
Outputs:
- token_scores: float32 [4096, 12], P(('grp', 'blk'))
- seq_scores: float32 [4, 12], P('grp')
The draws below stay inside these ranges and needn't reach their ends.
Inputs may be any that keep to these rules, and one draw needn't show every extreme that they name: `pair_query`: each query id appears exactly 32 times. `segment_ids`: never falling; each sequence has 1 to 2048 tokens, one exactly 2048.
All inputs are finite; a program needn't handle non-finite values.
Results may differ from the reference program's by a relative error of at most 0.0003.
Values may be sent and summed in bfloat16 or wider, within the bound.
A program may use at most 192 MiB of HBM per device.

```python
import math
import jax
import jax.numpy as jnp
import numpy as np
from jax import lax

D = 8192
FF = 28672
RANK = 32
QUERIES = 12
SEQ_LEN = 2048
PAIRS = 384
TOKENS = 4096
SEQS = 4


def draw_pair_query(key, part):
    order = jax.random.permutation(key, QUERIES * RANK)
    return (order // RANK).astype(jnp.int32)


def levels(stream_key, shape, cuts, least, high):
    level, own = 1.0, jax.random.fold_in(stream_key, 6)
    for dim, blocks in cuts:
        steps = jnp.exp(jax.random.uniform(jax.random.fold_in(own, dim), (blocks,), jnp.float32, least / len(cuts), high / len(cuts)))
        level = level * jnp.repeat(steps, shape[dim] // blocks).reshape([-1 if axis == dim else 1 for axis in range(len(shape))])
    return level


def length_profile(amount, total, bound, skew):
    loads = [(1 << 20) // math.isqrt(rank ** skew) + 1 for rank in range(2, amount + 1)]
    surplus, given = total - bound - (amount - 1), [1] * (amount - 1)
    while surplus > 0:
        free = [i for i in range(amount - 1) if given[i] < bound]
        pool, remaining = sum([loads[i] for i in free]), surplus
        for i in free:
            more = min(bound - given[i], max(1, remaining * loads[i] // pool), surplus)
            given[i] = given[i] + more
            surplus = surplus - more
    return np.array([bound] + given)


def uneven(key, count, total, bound, slope):
    if count == 2:
        one = jax.random.randint(key, (), max(1, total - bound), min(bound, total - 1) + 1)
        return jnp.stack([one, total - one])
    sizes = jnp.asarray(length_profile(count, total, bound, slope), jnp.int32)
    twos = (count - 1) // 2
    donor, taker = sizes[1:1 + 2 * twos:2], sizes[2:2 + 2 * twos:2]
    margin = jnp.minimum(donor - 1, bound - taker)
    shifted = jax.random.randint(jax.random.fold_in(key, 1), (twos,), 0, 1 << 20) % (margin + 1)
    sizes = sizes.at[1:1 + 2 * twos:2].set(donor - shifted).at[2:2 + 2 * twos:2].set(taker + shifted)
    return sizes[jax.random.permutation(jax.random.fold_in(key, 2), count)]


def scatter_about(stream_key, shape, deviation, bound, split=(), held_as=jnp.bfloat16):
    result = deviation * jax.random.normal(stream_key, shape, jnp.float32)
    if split:
        result = result * levels(stream_key, shape, split, -0.22, 0.18)
    return jnp.clip(result, -bound, bound).astype(held_as)


def setup_inputs(seed: int = 0, part: int = 0) -> dict:
    key_of = jax.random.split(jax.random.key(seed), 6)
    part_splits = jax.random.split(jax.random.fold_in(key_of[5], part), 6)
    activations = scatter_about(part_splits[0], (TOKENS, D), 1.0, 6.0, ((0, 32),))
    out_grads = scatter_about(part_splits[1], (TOKENS, FF), 1.0, 6.0, ((0, 32),))
    query_factors = scatter_about(key_of[2], (PAIRS, FF + D), ((RANK * FF * D) ** -0.25), 0.046875, ((0, 32),))
    pair_query = draw_pair_query(jax.random.fold_in(key_of[5], 71), part)
    segment_ids = jnp.searchsorted(jnp.cumsum(uneven(part_splits[4], SEQS, TOKENS, SEQ_LEN, 1)), jnp.arange(TOKENS), side="right").astype(jnp.int32)
    return dict(activations=activations, out_grads=out_grads, query_factors=query_factors, pair_query=pair_query, segment_ids=segment_ids)


def reference(activations, out_grads, query_factors, pair_query, segment_ids):
    out_side = query_factors[:, :FF]
    in_side = query_factors[:, FF:]
    out_proj = jnp.dot(out_grads, out_side.T, preferred_element_type=jnp.float32)
    in_proj = jnp.dot(activations, in_side.T, preferred_element_type=jnp.float32)
    owner = (pair_query[:, None] == jnp.arange(QUERIES, dtype=jnp.int32)[None, :]).astype(jnp.float32)
    token_scores = jnp.dot(out_proj * in_proj, owner, precision=lax.Precision.HIGHEST)
    member = (segment_ids[:, None] == jnp.arange(SEQS, dtype=jnp.int32)[None, :]).astype(jnp.float32)
    counts = lax.optimization_barrier(jnp.sum(member, axis=0))
    totals = jnp.dot(member.T, token_scores, precision=lax.Precision.HIGHEST)
    seq_scores = totals / jnp.sqrt(counts)[:, None]
    return (token_scores, seq_scores)
```

```python
import jax
import jax.numpy as jnp
from jax import lax
from jax.sharding import PartitionSpec as P

QUERIES = 12
SEQ_LEN = 2048


def pair_products(activations, out_grads, piece):
    width = out_grads.shape[1]
    numbers = (((1,), (1,)), ((), ()))
    out_proj = lax.dot_general(
        out_grads, piece[:, :width], numbers, preferred_element_type=jnp.float32
    )
    in_proj = lax.dot_general(
        activations, piece[:, width:], numbers, preferred_element_type=jnp.float32
    )
    return out_proj * in_proj


def local(activations, out_grads, query_factors, pair_query, segment_ids):
    n = lax.axis_size("blk")
    me = lax.axis_index("blk")
    core = lax.rem(me, 2)
    rows = query_factors.shape[0]
    swap = [(i, i ^ 1) for i in range(n)]
    groups = [list(range(0, n, 2)), list(range(1, n, 2))]
    gathered = lax.all_gather(query_factors, "blk", axis=0, tiled=True, axis_index_groups=groups)
    other_acts = lax.ppermute(activations, "blk", swap)
    other_grads = lax.ppermute(out_grads, "blk", swap)
    mine = lax.dynamic_index_in_dim(pair_query.reshape(n // 2, 2, rows), core, axis=1, keepdims=False)
    owner = (mine.reshape(-1)[:, None] == jnp.arange(QUERIES, dtype=jnp.int32)[None, :]).astype(
        jnp.float32
    )
    other_part = jnp.dot(
        pair_products(other_acts, other_grads, gathered), owner, precision=lax.Precision.HIGHEST
    )
    back = lax.ppermute(other_part, "blk", swap)
    token_scores = back + jnp.dot(
        pair_products(activations, out_grads, gathered), owner, precision=lax.Precision.HIGHEST
    )
    seq_total = 2 * activations.shape[0] * n // SEQ_LEN
    member = (segment_ids[:, None] == jnp.arange(seq_total, dtype=jnp.int32)[None, :]).astype(
        jnp.float32
    )
    partial_sums = jnp.dot(member.T, token_scores, precision=lax.Precision.HIGHEST)
    partial_counts = jnp.sum(member, axis=0)
    totals, counts = lax.psum((partial_sums, partial_counts), "blk")
    seq_scores = totals / jnp.sqrt(counts)[:, None]
    return (token_scores, seq_scores)


def solution(mesh):
    in_specs = (
        P(("grp", "blk"), None),
        P(("grp", "blk"), None),
        P("blk", None),
        P(),
        P(("grp", "blk")),
    )
    out_specs = (P(("grp", "blk"), None), P("grp", None))
    return jax.shard_map(local, mesh=mesh, in_specs=in_specs, out_specs=out_specs, check_vma=False)
```

```python
import jax
import jax.numpy as jnp
from jax import lax
from jax.experimental import pallas as pl
from jax.experimental.pallas import tpu as pltpu
from jax.sharding import PartitionSpec as P

QUERIES = 12
SEQ_LEN = 2048


def pair_products(activations, out_grads, piece):
    width = out_grads.shape[1]
    numbers = (((1,), (1,)), ((), ()))
    out_proj = lax.dot_general(
        out_grads, piece[:, :width], numbers, preferred_element_type=jnp.float32
    )
    in_proj = lax.dot_general(
        activations, piece[:, width:], numbers, preferred_element_type=jnp.float32
    )
    return out_proj * in_proj


def local(activations, out_grads, query_factors, pair_query, segment_ids):
    n = lax.axis_size("blk")
    me = lax.axis_index("blk")
    core = lax.rem(me, 2)
    rows = query_factors.shape[0]
    swap = [(i, i ^ 1) for i in range(n)]
    groups = [list(range(0, n, 2)), list(range(1, n, 2))]
    gathered = lax.all_gather(query_factors, "blk", axis=0, tiled=True, axis_index_groups=groups)
    other_acts = lax.ppermute(activations, "blk", swap)
    other_grads = lax.ppermute(out_grads, "blk", swap)
    mine = lax.dynamic_index_in_dim(pair_query.reshape(n // 2, 2, rows), core, axis=1, keepdims=False)
    owner = (mine.reshape(-1)[:, None] == jnp.arange(QUERIES, dtype=jnp.int32)[None, :]).astype(
        jnp.float32
    )
    other_part = jnp.dot(
        pair_products(other_acts, other_grads, gathered), owner, precision=lax.Precision.HIGHEST
    )
    back = lax.ppermute(other_part, "blk", swap)
    token_scores = back + jnp.dot(
        pair_products(activations, out_grads, gathered), owner, precision=lax.Precision.HIGHEST
    )
    seq_total = 2 * activations.shape[0] * n // SEQ_LEN
    member = (segment_ids[:, None] == jnp.arange(seq_total, dtype=jnp.int32)[None, :]).astype(
        jnp.float32
    )
    partial_sums = jnp.dot(member.T, token_scores, precision=lax.Precision.HIGHEST)
    partial_counts = jnp.sum(member, axis=0)
    totals, counts = lax.psum((partial_sums, partial_counts), "blk")
    seq_scores = totals / jnp.sqrt(counts)[:, None]
    return (token_scores, seq_scores)


MESH = pl.DeviceIdType.MESH
SUB = 8
LANES = 128
CHUNK = 1024
LAG = 2
DEPTH_PLANE = 2


def depth_of(mesh):
    sizes = dict(mesh.shape)
    if sizes.get("grp") != 1 or sizes["blk"] % 8:
        return 0
    devices = mesh.devices.reshape(-1)
    first = devices[0].coords
    for i, d in enumerate(devices):
        at = tuple(c - f for c, f in zip(d.coords, first))
        if at != ((i // 2) % 2, (i // 4) % 2, i // 8) or d.core_on_chip != i % 2:
            return 0
    return sizes["blk"] // 8


def kernel(nz, kc, seqs, half_out, slabs, acts, grads, ids, owner, ts_out, seq_out,
           buf, tok_l, tok_r, acc, ids2, part, part_in, sums, plane_in, line, line_in,
           recv_sem, send_sem, tok_sem, tok_send, own_sem, ids_sem, back_sem, plane_sem, line_sem):
    me = lax.axis_index("blk")
    core = lax.rem(me, 2)
    chip = me // 2
    x, y, z = lax.rem(chip, 2), lax.rem(chip // 2, 2), chip // 4
    tokens = acts.shape[0]
    width = slabs.shape[2]
    chunks = width // kc
    out_chunks = half_out // kc
    half_in = width - half_out
    chips = 4 * nz

    def dev(i):
        return {"blk": i}

    def place(cx, cy, cz, cc):
        return cz * 8 + cy * 4 + cx * 2 + cc

    sibling = place(x, y, z, 1 - core)
    to_x = place(1 - x, y, z, core)
    to_y = place(x, 1 - y, z, core)
    to_up = place(x, y, jnp.minimum(z + 1, nz - 1), core)
    to_down = place(x, y, jnp.maximum(z - 1, 0), core)

    local = [
        pltpu.make_async_copy(slabs, buf.at[chip], own_sem.at[0]),
        pltpu.make_async_copy(grads.at[:, :half_out], tok_l.at[:tokens, :half_out], own_sem.at[1]),
        pltpu.make_async_copy(grads.at[:, half_out:], tok_r.at[:tokens, :half_out], own_sem.at[2]),
        pltpu.make_async_copy(acts.at[:, :half_in], tok_l.at[:tokens, half_out:], own_sem.at[3]),
        pltpu.make_async_copy(acts.at[:, half_in:], tok_r.at[:tokens, half_out:], own_sem.at[4]),
    ]
    for copy in local:
        copy.start()

    barrier = pltpu.get_barrier_semaphore()
    for k in range(1, 8):
        pl.semaphore_signal(barrier, inc=1, device_id=dev(z * 8 + lax.rem(lax.rem(me, 8) + k, 8)), device_id_type=MESH)
    for k in range(1, nz):
        pl.semaphore_signal(barrier, inc=1, device_id=dev(lax.rem(me + 8 * k, 8 * nz)), device_id_type=MESH)
    pl.semaphore_wait(barrier, 7 + nz - 1)

    acc[...] = jnp.zeros_like(acc)
    local[0].wait()

    def ids_copy():
        return pltpu.make_async_remote_copy(
            src_ref=ids, dst_ref=ids2, send_sem=ids_sem.at[0], recv_sem=ids_sem.at[1],
            device_id=dev(sibling), device_id_type=MESH)

    def token_copies(c, kind):
        source, half, base = ((grads, half_out, 0), (acts, half_in, half_out))[kind]
        at = pl.multiple_of(c * kc, LANES)
        rel = pl.multiple_of(at - base, LANES)
        other = pl.multiple_of(rel + half, LANES)
        return [
            pltpu.make_async_remote_copy(
                src_ref=source.at[:, pl.ds(begin, kc)],
                dst_ref=tok.at[pl.ds(tokens, tokens), pl.ds(at, kc)],
                send_sem=tok_send.at[side, c], recv_sem=tok_sem.at[side, c],
                device_id=dev(sibling), device_id_type=MESH)
            for side, (begin, tok) in enumerate(((rel, tok_l), (other, tok_r)))
        ]

    def start_tokens(c):
        for kind, test in ((0, c < out_chunks), (1, c >= out_chunks)):
            @pl.when(test)
            def _():
                for copy in token_copies(c, kind):
                    copy.start()

    def piece(s, c, way, target):
        view = buf.at[s, :, :, pl.ds(pl.multiple_of(c * kc, LANES), kc)]
        return pltpu.make_async_remote_copy(
            src_ref=view, dst_ref=view, send_sem=send_sem.at[way, c], recv_sem=recv_sem.at[s, c],
            device_id=dev(target), device_id_type=MESH)

    def is_plane_first(c):
        k = lax.rem(c, 9)
        return jnp.logical_or(k == 3, k == 7)

    def event(zs, pos, t):
        gap = jnp.abs(z - zs)
        hops = gap + (0, 1, 1, 2)[pos]
        c = t - LAG * hops
        sx, sy = (x, 1 - x, x, 1 - x)[pos], (y, y, 1 - y, 1 - y)[pos]
        s = zs * 4 + sy * 2 + sx

        @pl.when(jnp.logical_and(c >= 0, c < chunks))
        def _():
            if pos == 0:
                @pl.when(gap > 0)
                def _():
                    piece(s, c, 0, to_x).wait_recv()
            else:
                piece(s, c, 0, to_x).wait_recv()
            plane_first = is_plane_first(c)
            odd = lax.rem(zs + c, 2) == 1
            along = plane_first if pos else jnp.bool_(True)
            flat = jnp.logical_or(jnp.logical_not(plane_first), gap == 0)

            @pl.when(along & (z >= zs) & (z < nz - 1))
            def _():
                piece(s, c, 2, to_up).start()

            @pl.when(along & (z <= zs) & (z > 0))
            def _():
                piece(s, c, 3, to_down).start()

            if pos in (0, 2):
                @pl.when(flat if pos == 0 else flat & odd)
                def _():
                    piece(s, c, 0, to_x).start()
            if pos in (0, 1):
                @pl.when(flat if pos == 0 else flat & jnp.logical_not(odd))
                def _():
                    piece(s, c, 1, to_y).start()

    def multiply(c):
        cols = pl.ds(pl.multiple_of(c * kc, LANES), kc)
        kind = jnp.where(c >= out_chunks, 1, 0)
        for side, tok in ((0, tok_l), (1, tok_r)):
            pltpu.make_async_copy(
                tok.at[pl.ds(tokens, tokens), cols], tok.at[pl.ds(tokens, tokens), cols], tok_sem.at[side, c]
            ).wait()
        rest = buf[:, 2, :, cols].reshape(chips * SUB, kc)
        for side, tok in ((0, tok_l), (1, tok_r)):
            rows = jnp.concatenate([buf[:, side, :, cols].reshape(chips * SUB, kc), rest], axis=0)
            acc[kind, side] += lax.dot_general(
                tok[:, cols], rows, (((1,), (1,)), ((), ())), preferred_element_type=jnp.float32)

    last = LAG * (nz - 1 + DEPTH_PLANE)
    ids_copy().start()

    @pl.loop(0, chunks + last)
    def _(t):
        for zs in range(nz):
            event(zs, 0, t)
        for pos in (1, 2, 3):
            for zs in range(nz):
                event(zs, pos, t)

        @pl.when(t < chunks)
        def _():
            start_tokens(t)

        @pl.when(t == last)
        def _():
            for copy in local[1:]:
                copy.wait()

        @pl.when(t >= last)
        def _():
            multiply(t - last)

    n_main = chips * SUB
    def joined(kind):
        left, right = acc[kind, 0], acc[kind, 1]
        main = left[:, :n_main] + right[:, :n_main]
        tail = left[:, n_main:] + pltpu.roll(right[:, n_main:], n_main - SUB // 2, 1)
        return jnp.concatenate([main, tail], axis=1)

    scores = jnp.dot(joined(0) * joined(1), owner[...], precision=lax.Precision.HIGHEST,
                     preferred_element_type=jnp.float32)
    part[...] = scores[tokens:]
    back = pltpu.make_async_remote_copy(
        src_ref=part, dst_ref=part_in, send_sem=back_sem.at[0], recv_sem=back_sem.at[1],
        device_id=dev(sibling), device_id_type=MESH)
    back.start()
    ids_copy().wait()
    seq_rows = sums.shape[0]
    lane = lax.broadcasted_iota(jnp.int32, (tokens, LANES), 1)
    mine = jnp.where(lane == QUERIES, 1.0, scores[:tokens])
    row = lax.broadcasted_iota(jnp.int32, (seq_rows, tokens), 0)

    def by_sequence(which, values):
        member = (row == which[...]).astype(jnp.float32)
        return jnp.dot(member, values, precision=lax.Precision.HIGHEST, preferred_element_type=jnp.float32)

    sums[...] = by_sequence(ids, mine) + by_sequence(ids2, scores[tokens:])
    spot = lax.rem(me, 8)

    def plane_copy(k):
        return pltpu.make_async_remote_copy(
            src_ref=sums, dst_ref=plane_in.at[k - 1], send_sem=plane_sem.at[0, k - 1], recv_sem=plane_sem.at[1, k - 1],
            device_id=dev(z * 8 + lax.rem(spot + k, 8)), device_id_type=MESH)

    for k in range(1, 8):
        plane_copy(k).start()
    back.wait()
    ts_out[...] = scores[:tokens] + part_in[...]
    for k in range(1, 8):
        plane_copy(k).wait()
    total = jnp.zeros((seq_rows, LANES), jnp.float32)
    own = sums[...]
    held = [own] + [plane_in[k - 1] for k in range(1, 8)]
    for i in range(8):
        k = lax.rem(spot - i + 8, 8)
        term = jnp.zeros_like(total)
        for j in range(8):
            term = jnp.where(k == j, held[j], term)
        total = total + term
    line[...] = total

    def line_copy(k):
        return pltpu.make_async_remote_copy(
            src_ref=line, dst_ref=line_in.at[k - 1], send_sem=line_sem.at[0, k - 1], recv_sem=line_sem.at[1, k - 1],
            device_id=dev(lax.rem(me + 8 * k, 8 * nz)), device_id_type=MESH)

    for k in range(1, nz):
        line_copy(k).start()
    for k in range(1, nz):
        line_copy(k).wait()
    held = [total] + [line_in[k - 1] for k in range(1, nz)]
    total = jnp.zeros_like(total)
    for i in range(nz):
        k = lax.rem(z - i + nz, nz)
        term = jnp.zeros_like(total)
        for j in range(nz):
            term = jnp.where(k == j, held[j], term)
        total = total + term
    seq_out[...] = total / jnp.sqrt(total[:, QUERIES:QUERIES + 1])

    def sent(way, c, n):
        view = buf.at[pl.ds(0, n), :, :, pl.ds(0, kc)]
        pltpu.make_async_remote_copy(
            src_ref=view, dst_ref=view, send_sem=send_sem.at[way, c], recv_sem=recv_sem.at[0, 0],
            device_id=dev(to_x), device_id_type=MESH).wait_send()

    @pl.loop(0, chunks)
    def _(c):
        plane_first = is_plane_first(c)
        for kind, test in ((0, jnp.logical_not(plane_first)), (1, plane_first)):
            for odd_c in (0, 1):
                n_odd = sum((zs + odd_c) % 2 for zs in range(nz))

                @pl.when(test & (lax.rem(c, 2) == odd_c))
                def _():
                    if kind == 0:
                        sent(0, c, nz + n_odd)
                        sent(1, c, nz + nz - n_odd)
                    else:
                        for own_odd in (0, 1):
                            @pl.when(lax.rem(z, 2) == own_odd)
                            def _():
                                n = (own_odd + odd_c) % 2
                                sent(0, c, 1 + n)
                                sent(1, c, 2 - n)
            for k in range(nz):
                @pl.when(test & (z == k))
                def _():
                    each = 4 if kind else 1
                    if k < nz - 1:
                        sent(2, c, each * (k + 1))
                    if k > 0:
                        sent(3, c, each * (nz - k))
        for kind, test in ((0, c < out_chunks), (1, c >= out_chunks)):
            @pl.when(test)
            def _():
                for copy in token_copies(c, kind):
                    copy.wait_send()


def routed(nz):
    def run(activations, out_grads, query_factors, pair_query, segment_ids):
        n = lax.axis_size("blk")
        chips = n // 2
        core = lax.rem(lax.axis_index("blk"), 2)
        rows = query_factors.shape[0]
        tokens, wide = out_grads.shape
        narrow = activations.shape[1]
        half_out, half_in = wide // 2, narrow // 2
        width = half_out + half_in
        seqs = 2 * tokens * n // SEQ_LEN
        left = jnp.concatenate([query_factors[:, :half_out], query_factors[:, wide:wide + half_in]], axis=1)
        right = jnp.concatenate([query_factors[:, half_out:wide], query_factors[:, wide + half_in:]], axis=1)
        slabs = jnp.stack([left[:SUB], right[:SUB], jnp.concatenate([left[SUB:], right[SUB:]], axis=0)])
        mine = lax.dynamic_index_in_dim(pair_query.reshape(chips, 2, rows), core, axis=1, keepdims=False)
        tail = jnp.pad(mine[:, SUB:], ((0, 0), (0, 2 * SUB - rows)), constant_values=-1)
        which = jnp.concatenate([mine[:, :SUB].reshape(-1), tail.reshape(-1)])
        owner = (which[:, None] == jnp.arange(LANES, dtype=jnp.int32)[None, :]).astype(jnp.float32)
        seq_rows = -(-seqs // SUB) * SUB
        chunks = width // CHUNK
        vmem, any_ = pl.BlockSpec(memory_space=pltpu.VMEM), pl.BlockSpec(memory_space=pl.ANY)
        f32 = jnp.float32
        dma = pltpu.SemaphoreType.DMA
        scores, seq = pl.pallas_call(
            lambda *refs: kernel(nz, CHUNK, seqs, half_out, *refs),
            name="routed_scores",
            out_shape=(jax.ShapeDtypeStruct((tokens, LANES), f32), jax.ShapeDtypeStruct((seq_rows, LANES), f32)),
            in_specs=[any_, any_, any_, vmem, vmem],
            out_specs=(vmem, vmem),
            scratch_shapes=[
                pltpu.VMEM((chips, 3, SUB, width), jnp.bfloat16),
                pltpu.VMEM((2 * tokens, width), jnp.bfloat16),
                pltpu.VMEM((2 * tokens, width), jnp.bfloat16),
                pltpu.VMEM((2, 2, 2 * tokens, 2 * chips * SUB), f32),
                pltpu.VMEM((1, tokens), jnp.int32),
                pltpu.VMEM((tokens, LANES), f32),
                pltpu.VMEM((tokens, LANES), f32),
                pltpu.VMEM((seq_rows, LANES), f32),
                pltpu.VMEM((7, seq_rows, LANES), f32),
                pltpu.VMEM((seq_rows, LANES), f32),
                pltpu.VMEM((nz - 1, seq_rows, LANES), f32),
                dma((chips, chunks)),
                dma((4, chunks)),
                dma((2, chunks)),
                dma((2, chunks)),
                dma((5,)),
                dma((2,)),
                dma((2,)),
                dma((2, 7)),
                dma((2, nz - 1)),
            ],
            compiler_params=pltpu.CompilerParams(
                collective_id=0, has_side_effects=True, vmem_limit_bytes=60 * 1024 * 1024),
        )(slabs, activations, out_grads, segment_ids.reshape(1, -1), owner)
        return scores[:, :QUERIES], seq[:seqs, :QUERIES]

    return run


def solution(mesh):
    nz = depth_of(mesh)
    in_specs = (
        P(("grp", "blk"), None),
        P(("grp", "blk"), None),
        P("blk", None),
        P(),
        P(("grp", "blk")),
    )
    out_specs = (P(("grp", "blk"), None), P("grp", None))
    return jax.shard_map(routed(nz) if nz > 1 else local, mesh=mesh, in_specs=in_specs, out_specs=out_specs, check_vma=False)
```

```python
import jax
import jax.numpy as jnp
from jax import lax
from jax.experimental import pallas as pl
from jax.experimental.pallas import tpu as pltpu
from jax.sharding import PartitionSpec as P

QUERIES = 12
SEQ_LEN = 2048


def pair_products(activations, out_grads, piece):
    width = out_grads.shape[1]
    numbers = (((1,), (1,)), ((), ()))
    out_proj = lax.dot_general(
        out_grads, piece[:, :width], numbers, preferred_element_type=jnp.float32
    )
    in_proj = lax.dot_general(
        activations, piece[:, width:], numbers, preferred_element_type=jnp.float32
    )
    return out_proj * in_proj


def local(activations, out_grads, query_factors, pair_query, segment_ids):
    n = lax.axis_size("blk")
    me = lax.axis_index("blk")
    core = lax.rem(me, 2)
    rows = query_factors.shape[0]
    swap = [(i, i ^ 1) for i in range(n)]
    groups = [list(range(0, n, 2)), list(range(1, n, 2))]
    gathered = lax.all_gather(query_factors, "blk", axis=0, tiled=True, axis_index_groups=groups)
    other_acts = lax.ppermute(activations, "blk", swap)
    other_grads = lax.ppermute(out_grads, "blk", swap)
    mine = lax.dynamic_index_in_dim(pair_query.reshape(n // 2, 2, rows), core, axis=1, keepdims=False)
    owner = (mine.reshape(-1)[:, None] == jnp.arange(QUERIES, dtype=jnp.int32)[None, :]).astype(
        jnp.float32
    )
    other_part = jnp.dot(
        pair_products(other_acts, other_grads, gathered), owner, precision=lax.Precision.HIGHEST
    )
    back = lax.ppermute(other_part, "blk", swap)
    token_scores = back + jnp.dot(
        pair_products(activations, out_grads, gathered), owner, precision=lax.Precision.HIGHEST
    )
    seq_total = 2 * activations.shape[0] * n // SEQ_LEN
    member = (segment_ids[:, None] == jnp.arange(seq_total, dtype=jnp.int32)[None, :]).astype(
        jnp.float32
    )
    partial_sums = jnp.dot(member.T, token_scores, precision=lax.Precision.HIGHEST)
    partial_counts = jnp.sum(member, axis=0)
    totals, counts = lax.psum((partial_sums, partial_counts), "blk")
    seq_scores = totals / jnp.sqrt(counts)[:, None]
    return (token_scores, seq_scores)


MESH = pl.DeviceIdType.MESH
SUB = 8
LANES = 128
CHUNK = 1024
LAG = 3
AHEAD = 5
PLANE_FIRST = (1, 5)
DEPTH_PLANE = 2


def depth_of(mesh):
    sizes = dict(mesh.shape)
    if sizes.get("grp") != 1 or sizes["blk"] % 8:
        return 0
    devices = mesh.devices.reshape(-1)
    first = devices[0].coords
    for i, d in enumerate(devices):
        at = tuple(c - f for c, f in zip(d.coords, first))
        if at != ((i // 2) % 2, (i // 4) % 2, i // 8) or d.core_on_chip != i % 2:
            return 0
    return sizes["blk"] // 8


def kernel(nz, kc, seqs, half_out, factors, tail, acts, grads, ids, owner, ts_out, seq_out,
           buf, tok_l, tok_r, acc, ids2, part, part_in, sums, plane_in, line, line_in,
           recv_sem, send_sem, tok_sem, tok_send, own_sem, ids_sem, back_sem, plane_sem, line_sem):
    me = lax.axis_index("blk")
    core = lax.rem(me, 2)
    chip = me // 2
    x, y, z = lax.rem(chip, 2), lax.rem(chip // 2, 2), chip // 4
    tokens = acts.shape[0]
    width = tail.shape[1]
    chunks = width // kc
    out_chunks = half_out // kc
    half_in = width - half_out
    chips = 4 * nz

    def dev(i):
        return {"blk": i}

    def place(cx, cy, cz, cc):
        return cz * 8 + cy * 4 + cx * 2 + cc

    sibling = place(x, y, z, 1 - core)
    to_x = place(1 - x, y, z, core)
    to_y = place(x, 1 - y, z, core)
    to_up = place(x, y, jnp.minimum(z + 1, nz - 1), core)
    to_down = place(x, y, jnp.maximum(z - 1, 0), core)

    local = [
        pltpu.make_async_copy(grads.at[:, :half_out], tok_l.at[:tokens, :half_out], own_sem.at[5]),
        pltpu.make_async_copy(grads.at[:, half_out:], tok_r.at[:tokens, :half_out], own_sem.at[6]),
        pltpu.make_async_copy(acts.at[:, :half_in], tok_l.at[:tokens, half_out:], own_sem.at[7]),
        pltpu.make_async_copy(acts.at[:, half_in:], tok_r.at[:tokens, half_out:], own_sem.at[8]),
    ]
    wide = 2 * half_out
    factor_copies = [pltpu.make_async_copy(tail, buf.at[chip, 2], own_sem.at[0])]
    for side in (0, 1):
        for k, (begin, at, size) in enumerate((
            (side * half_out, 0, half_out), (wide + side * half_in, half_out, half_in))):
            factor_copies.append(pltpu.make_async_copy(
                factors.at[:SUB, begin:begin + size], buf.at[chip, side, :, at:at + size],
                own_sem.at[1 + 2 * side + k]))
    for copy in factor_copies + local:
        copy.start()

    barrier = pltpu.get_barrier_semaphore()
    for k in range(1, 8):
        pl.semaphore_signal(barrier, inc=1, device_id=dev(z * 8 + lax.rem(lax.rem(me, 8) + k, 8)), device_id_type=MESH)
    for k in range(1, nz):
        pl.semaphore_signal(barrier, inc=1, device_id=dev(lax.rem(me + 8 * k, 8 * nz)), device_id_type=MESH)
    pl.semaphore_wait(barrier, 7 + nz - 1)

    acc[...] = jnp.zeros_like(acc)
    for copy in factor_copies:
        copy.wait()

    def ids_copy():
        return pltpu.make_async_remote_copy(
            src_ref=ids, dst_ref=ids2, send_sem=ids_sem.at[0], recv_sem=ids_sem.at[1],
            device_id=dev(sibling), device_id_type=MESH)

    def token_copies(c, kind):
        source, half, base = ((grads, half_out, 0), (acts, half_in, half_out))[kind]
        at = pl.multiple_of(c * kc, LANES)
        rel = pl.multiple_of(at - base, LANES)
        other = pl.multiple_of(rel + half, LANES)
        return [
            pltpu.make_async_remote_copy(
                src_ref=source.at[:, pl.ds(begin, kc)],
                dst_ref=tok.at[pl.ds(tokens, tokens), pl.ds(at, kc)],
                send_sem=tok_send.at[side, c], recv_sem=tok_sem.at[side, c],
                device_id=dev(sibling), device_id_type=MESH)
            for side, (begin, tok) in enumerate(((rel, tok_l), (other, tok_r)))
        ]

    def start_tokens(c):
        for kind, test in ((0, c < out_chunks), (1, c >= out_chunks)):
            @pl.when(test)
            def _():
                for copy in token_copies(c, kind):
                    copy.start()

    def piece(s, c, way, target):
        view = buf.at[s, :, :, pl.ds(pl.multiple_of(c * kc, LANES), kc)]
        return pltpu.make_async_remote_copy(
            src_ref=view, dst_ref=view, send_sem=send_sem.at[way, c], recv_sem=recv_sem.at[s, c],
            device_id=dev(target), device_id_type=MESH)

    def is_plane_first(c):
        k = lax.rem(c, 9)
        hit = jnp.bool_(False)
        for at in PLANE_FIRST:
            hit = hit | (k == at)
        return hit

    def event(zs, pos, t):
        gap = jnp.abs(z - zs)
        hops = gap + (0, 1, 1, 2)[pos]
        c = t - LAG * hops
        if pos == 0:
            c = jnp.where(gap == 0, c + AHEAD, c)
        sx, sy = (x, 1 - x, x, 1 - x)[pos], (y, y, 1 - y, 1 - y)[pos]
        s = zs * 4 + sy * 2 + sx

        @pl.when(jnp.logical_and(c >= 0, c < chunks))
        def _():
            if pos == 0:
                @pl.when(gap > 0)
                def _():
                    piece(s, c, 0, to_x).wait_recv()
            else:
                piece(s, c, 0, to_x).wait_recv()
            plane_first = is_plane_first(c)
            odd = lax.rem(zs + c, 2) == 1
            along = plane_first if pos else jnp.bool_(True)
            flat = jnp.logical_or(jnp.logical_not(plane_first), gap == 0)

            @pl.when(along & (z >= zs) & (z < nz - 1))
            def _():
                piece(s, c, 2, to_up).start()

            @pl.when(along & (z <= zs) & (z > 0))
            def _():
                piece(s, c, 3, to_down).start()

            if pos in (0, 2):
                @pl.when(flat if pos == 0 else flat & odd)
                def _():
                    piece(s, c, 0, to_x).start()
            if pos in (0, 1):
                @pl.when(flat if pos == 0 else flat & jnp.logical_not(odd))
                def _():
                    piece(s, c, 1, to_y).start()

    def multiply(c):
        cols = pl.ds(pl.multiple_of(c * kc, LANES), kc)
        kind = jnp.where(c >= out_chunks, 1, 0)
        for side, tok in ((0, tok_l), (1, tok_r)):
            pltpu.make_async_copy(
                tok.at[pl.ds(tokens, tokens), cols], tok.at[pl.ds(tokens, tokens), cols], tok_sem.at[side, c]
            ).wait()
        rest = buf[:, 2, :, cols].reshape(chips * SUB, kc)
        for side, tok in ((0, tok_l), (1, tok_r)):
            rows = jnp.concatenate([buf[:, side, :, cols].reshape(chips * SUB, kc), rest], axis=0)
            acc[kind, side] += lax.dot_general(
                tok[:, cols], rows, (((1,), (1,)), ((), ())), preferred_element_type=jnp.float32)

    last = LAG * (nz - 1 + DEPTH_PLANE)
    ids_copy().start()

    @pl.loop(0, chunks + last + AHEAD)
    def _(step):
        t = step - AHEAD
        for zs in range(nz):
            event(zs, 0, t)
        for pos in (1, 2, 3):
            for zs in range(nz):
                event(zs, pos, t)

        @pl.when((t >= 0) & (t < chunks))
        def _():
            start_tokens(t)

        @pl.when(t == last)
        def _():
            for copy in local:
                copy.wait()

        @pl.when(t >= last)
        def _():
            multiply(t - last)

    n_main = chips * SUB
    def joined(kind):
        left, right = acc[kind, 0], acc[kind, 1]
        main = left[:, :n_main] + right[:, :n_main]
        tail = left[:, n_main:] + pltpu.roll(right[:, n_main:], n_main - SUB // 2, 1)
        return jnp.concatenate([main, tail], axis=1)

    scores = jnp.dot(joined(0) * joined(1), owner[...], precision=lax.Precision.HIGHEST,
                     preferred_element_type=jnp.float32)
    part[...] = scores[tokens:]
    back = pltpu.make_async_remote_copy(
        src_ref=part, dst_ref=part_in, send_sem=back_sem.at[0], recv_sem=back_sem.at[1],
        device_id=dev(sibling), device_id_type=MESH)
    back.start()
    ids_copy().wait()
    seq_rows = sums.shape[0]
    lane = lax.broadcasted_iota(jnp.int32, (tokens, LANES), 1)
    mine = jnp.where(lane == QUERIES, 1.0, scores[:tokens])
    row = lax.broadcasted_iota(jnp.int32, (seq_rows, tokens), 0)

    def by_sequence(which, values):
        member = (row == which[...]).astype(jnp.float32)
        return jnp.dot(member, values, precision=lax.Precision.HIGHEST, preferred_element_type=jnp.float32)

    sums[...] = by_sequence(ids, mine) + by_sequence(ids2, scores[tokens:])
    spot = lax.rem(me, 8)

    def plane_copy(k):
        return pltpu.make_async_remote_copy(
            src_ref=sums, dst_ref=plane_in.at[k - 1], send_sem=plane_sem.at[0, k - 1], recv_sem=plane_sem.at[1, k - 1],
            device_id=dev(z * 8 + lax.rem(spot + k, 8)), device_id_type=MESH)

    for k in range(1, 8):
        plane_copy(k).start()
    back.wait()
    ts_out[...] = jnp.transpose(scores[:tokens] + part_in[...])[:QUERIES]
    for k in range(1, 8):
        plane_copy(k).wait()
    total = jnp.zeros((seq_rows, LANES), jnp.float32)
    own = sums[...]
    held = [own] + [plane_in[k - 1] for k in range(1, 8)]
    for i in range(8):
        k = lax.rem(spot - i + 8, 8)
        term = jnp.zeros_like(total)
        for j in range(8):
            term = jnp.where(k == j, held[j], term)
        total = total + term
    line[...] = total

    def line_copy(k):
        return pltpu.make_async_remote_copy(
            src_ref=line, dst_ref=line_in.at[k - 1], send_sem=line_sem.at[0, k - 1], recv_sem=line_sem.at[1, k - 1],
            device_id=dev(lax.rem(me + 8 * k, 8 * nz)), device_id_type=MESH)

    for k in range(1, nz):
        line_copy(k).start()
    for k in range(1, nz):
        line_copy(k).wait()
    held = [total] + [line_in[k - 1] for k in range(1, nz)]
    total = jnp.zeros_like(total)
    for i in range(nz):
        k = lax.rem(z - i + nz, nz)
        term = jnp.zeros_like(total)
        for j in range(nz):
            term = jnp.where(k == j, held[j], term)
        total = total + term
    seq_out[...] = (total / jnp.sqrt(total[:, QUERIES:QUERIES + 1]))[:seqs, :QUERIES]

    def sent(way, c, n):
        view = buf.at[pl.ds(0, n), :, :, pl.ds(0, kc)]
        pltpu.make_async_remote_copy(
            src_ref=view, dst_ref=view, send_sem=send_sem.at[way, c], recv_sem=recv_sem.at[0, 0],
            device_id=dev(to_x), device_id_type=MESH).wait_send()

    @pl.loop(0, chunks)
    def _(c):
        plane_first = is_plane_first(c)
        for kind, test in ((0, jnp.logical_not(plane_first)), (1, plane_first)):
            for odd_c in (0, 1):
                n_odd = sum((zs + odd_c) % 2 for zs in range(nz))

                @pl.when(test & (lax.rem(c, 2) == odd_c))
                def _():
                    if kind == 0:
                        sent(0, c, nz + n_odd)
                        sent(1, c, nz + nz - n_odd)
                    else:
                        for own_odd in (0, 1):
                            @pl.when(lax.rem(z, 2) == own_odd)
                            def _():
                                n = (own_odd + odd_c) % 2
                                sent(0, c, 1 + n)
                                sent(1, c, 2 - n)
            for k in range(nz):
                @pl.when(test & (z == k))
                def _():
                    each = 4 if kind else 1
                    if k < nz - 1:
                        sent(2, c, each * (k + 1))
                    if k > 0:
                        sent(3, c, each * (nz - k))
        for kind, test in ((0, c < out_chunks), (1, c >= out_chunks)):
            @pl.when(test)
            def _():
                for copy in token_copies(c, kind):
                    copy.wait_send()


def routed(nz):
    def run(activations, out_grads, query_factors, pair_query, segment_ids):
        n = lax.axis_size("blk")
        chips = n // 2
        core = lax.rem(lax.axis_index("blk"), 2)
        rows = query_factors.shape[0]
        tokens, wide = out_grads.shape
        narrow = activations.shape[1]
        half_out, half_in = wide // 2, narrow // 2
        width = half_out + half_in
        seqs = 2 * tokens * n // SEQ_LEN
        low = query_factors[SUB:]
        left = jnp.concatenate([low[:, :half_out], low[:, wide:wide + half_in]], axis=1)
        right = jnp.concatenate([low[:, half_out:wide], low[:, wide + half_in:]], axis=1)
        rest = jnp.concatenate([left, right], axis=0)
        mine = lax.dynamic_index_in_dim(pair_query.reshape(chips, 2, rows), core, axis=1, keepdims=False)
        tail = jnp.pad(mine[:, SUB:], ((0, 0), (0, 2 * SUB - rows)), constant_values=-1)
        which = jnp.concatenate([mine[:, :SUB].reshape(-1), tail.reshape(-1)])
        owner = (which[:, None] == jnp.arange(LANES, dtype=jnp.int32)[None, :]).astype(jnp.float32)
        seq_rows = -(-seqs // SUB) * SUB
        chunks = width // CHUNK
        vmem, any_ = pl.BlockSpec(memory_space=pltpu.VMEM), pl.BlockSpec(memory_space=pl.ANY)
        f32 = jnp.float32
        dma = pltpu.SemaphoreType.DMA
        scores, seq = pl.pallas_call(
            lambda *refs: kernel(nz, CHUNK, seqs, half_out, *refs),
            name="routed_scores",
            out_shape=(jax.ShapeDtypeStruct((QUERIES, tokens), f32), jax.ShapeDtypeStruct((seqs, QUERIES), f32)),
            in_specs=[any_, any_, any_, any_, vmem, vmem],
            out_specs=(vmem, vmem),
            scratch_shapes=[
                pltpu.VMEM((chips, 3, SUB, width), jnp.bfloat16),
                pltpu.VMEM((2 * tokens, width), jnp.bfloat16),
                pltpu.VMEM((2 * tokens, width), jnp.bfloat16),
                pltpu.VMEM((2, 2, 2 * tokens, 2 * chips * SUB), f32),
                pltpu.VMEM((1, tokens), jnp.int32),
                pltpu.VMEM((tokens, LANES), f32),
                pltpu.VMEM((tokens, LANES), f32),
                pltpu.VMEM((seq_rows, LANES), f32),
                pltpu.VMEM((7, seq_rows, LANES), f32),
                pltpu.VMEM((seq_rows, LANES), f32),
                pltpu.VMEM((nz - 1, seq_rows, LANES), f32),
                dma((chips, chunks)),
                dma((4, chunks)),
                dma((2, chunks)),
                dma((2, chunks)),
                dma((9,)),
                dma((2,)),
                dma((2,)),
                dma((2, 7)),
                dma((2, nz - 1)),
            ],
            compiler_params=pltpu.CompilerParams(
                collective_id=0, has_side_effects=True, vmem_limit_bytes=60 * 1024 * 1024),
        )(query_factors, rest, activations, out_grads, segment_ids.reshape(1, -1), owner)
        return scores.T, seq

    return run


def solution(mesh):
    nz = depth_of(mesh)
    in_specs = (
        P(("grp", "blk"), None),
        P(("grp", "blk"), None),
        P("blk", None),
        P(),
        P(("grp", "blk")),
    )
    out_specs = (P(("grp", "blk"), None), P("grp", None))
    return jax.shard_map(routed(nz) if nz > 1 else local, mesh=mesh, in_specs=in_specs, out_specs=out_specs, check_vma=False)
```
